32 devices in a mesh: gx: 8 (over z, x), gy: 4 (over y, core).
Axes of the slice: x: 2, y: 2, z: 4, core: 2. Of those that a mesh axis runs over, the one named last changes fastest.
Arguments:
- level_set: float32 [256, 128, 128], P('gx', 'gy'), may hold values from -6 to 6
- sensitivity: float32 [256, 128, 128], P('gx', 'gy'), may hold values from -6 to 6
- smooth_taps: float32 [25], replicated, may hold values from 0.1 to 0.3
- slope_taps: float32 [25], replicated, as said below
- band: int32 [16, 8, 4], P('gx', 'gy'), may hold values from 0 to 1
- time_step: float32 [1], replicated, may hold values from 0.05 to 0.15
Outputs:
- updated: float32 [256, 128, 128], P('gx', 'gy')
The draws below stay inside these ranges and needn't reach their ends.
Inputs may be any that keep to these rules, and one draw needn't show every extreme that they name: slope_taps[24 - k] = -slope_taps[k]; the middle tap is zero.
All inputs are finite; a program needn't handle non-finite values.
Results may differ from the reference program's by a relative error of at most 0.00002.
Values sent between devices are 32-bit elements; how exact they have to be, the bound alone decides.
A program may use at most 64 MiB of HBM per device.

```python
import math
import jax
import jax.numpy as jnp
from jax import lax

NZ = 128
TAPS = 25
BX = 16
BY = 16
BZ = 32
UPDATES = 2
NX = 256
NY = 128


def draw_slope_taps(key, part):
    halves = jax.random.normal(key, (TAPS // 2,), jnp.float32) * 0.3
    return jnp.concatenate([-halves[::-1], jnp.zeros((1,), jnp.float32), halves])


def draw_band(key, part):
    shape = (NX // BX, NY // BY, NZ // BZ)
    rolls = jax.random.randint(key, shape, 0, 8)
    levels = jax.random.randint(jax.random.fold_in(key, 1), (shape[0], 1, 1), 2, 9)
    return (rolls < levels).astype(jnp.int32)


def shard_levels(rng, extent, cuts, low, top_value):
    def one(axis_at, blocks):
        draws = jax.random.uniform(jax.random.fold_in(jax.random.fold_in(rng, 6), axis_at), (blocks,), jnp.float32, low / len(cuts), top_value / len(cuts))
        return jnp.repeat(jnp.exp(draws), extent[axis_at] // blocks).reshape((-1,) + (1,) * (len(extent) - axis_at - 1))

    loudness = one(*cuts[0])
    for cut in cuts[1:]:
        loudness = loudness * one(*cut)
    return loudness


def bell_draw(own_key, shape, width, bound, split=(), held_as=jnp.bfloat16):
    values = jax.random.normal(own_key, shape, jnp.float32) * width
    if len(split) > 0:
        values = shard_levels(own_key, shape, split, -0.22, 0.18) * values
    return jnp.clip(values, min=-bound, max=bound).astype(held_as)


def setup_inputs(seed: int = 0) -> dict:
    seeds = jax.random.split(jax.random.key(seed), 7)
    level_set = bell_draw(seeds[0], (NX, NY, NZ), 1.0, 6.0, ((0, 8), (1, 4)), jnp.float32)
    sensitivity = bell_draw(seeds[1], (NX, NY, NZ), 1.0, 6.0, ((0, 8), (1, 4)), jnp.float32)
    smooth_taps = jnp.clip(jnp.exp(jax.random.uniform(seeds[2], (TAPS,), jnp.float32, math.log(0.1), math.log(0.3))), 0.1, 0.3)
    slope_taps = draw_slope_taps(jax.random.fold_in(seeds[6], 71), 0)
    band = draw_band(jax.random.fold_in(seeds[6], 71), 0)
    time_step = jnp.clip(jax.random.uniform(seeds[5], (1,), jnp.float32, 0.05, 0.15), 0.05, 0.15)
    return {"level_set": level_set, "sensitivity": sensitivity, "smooth_taps": smooth_taps, "slope_taps": slope_taps, "band": band, "time_step": time_step}


def filt(field, taps, axis):
    length = field.shape[axis]
    widths = [(0, 0)] * field.ndim
    widths[axis] = (12, 12)
    padded = jnp.pad(field, widths)
    summed = taps[0] * lax.slice_in_dim(padded, 0, length, axis=axis)
    for offset in range(1, 25):
        summed = summed + taps[offset] * lax.slice_in_dim(padded, offset, offset + length, axis=axis)
    return summed

def reference(level_set, sensitivity, smooth_taps, slope_taps, band, time_step):
    velocity = filt(filt(filt(sensitivity, smooth_taps, 2), smooth_taps, 0), smooth_taps, 1)
    padded_v = jnp.pad(velocity, 1)
    speed = (padded_v[1:-1, 1:-1, 1:-1] + padded_v[2:, 1:-1, 1:-1] + padded_v[:-2, 1:-1, 1:-1] + padded_v[1:-1, 2:, 1:-1] + padded_v[1:-1, :-2, 1:-1] + padded_v[1:-1, 1:-1, 2:] + padded_v[1:-1, 1:-1, :-2]) / 7.0
    blocks_x, blocks_y, blocks_z = band.shape
    mask = jnp.broadcast_to(band.astype(jnp.float32)[:, None, :, None, :, None], (blocks_x, BX, blocks_y, BY, blocks_z, BZ)).reshape(level_set.shape)
    step_size = time_step[0]
    phi = level_set
    for update_index in range(UPDATES):
        depth_smooth = filt(phi, smooth_taps, 2)
        depth_slope = filt(phi, slope_taps, 2)
        cross_smooth = filt(depth_smooth, smooth_taps, 0)
        cross_slope = filt(depth_smooth, slope_taps, 0)
        third_smooth = filt(depth_slope, smooth_taps, 0)
        grad_x = filt(cross_slope, smooth_taps, 1)
        grad_y = filt(cross_smooth, slope_taps, 1)
        grad_z = filt(third_smooth, smooth_taps, 1)
        magnitude = jnp.sqrt(grad_x * grad_x + grad_y * grad_y + grad_z * grad_z + 1.0)
        normal_x = jnp.pad(grad_x / magnitude, ((1, 1), (0, 0), (0, 0)))
        normal_y = jnp.pad(grad_y / magnitude, ((0, 0), (1, 1), (0, 0)))
        normal_z = jnp.pad(grad_z / magnitude, ((0, 0), (0, 0), (1, 1)))
        curvature = 0.5 * (normal_x[2:] - normal_x[:-2]) + 0.5 * (normal_y[:, 2:] - normal_y[:, :-2]) + 0.5 * (normal_z[:, :, 2:] - normal_z[:, :, :-2])
        phi = phi - mask * step_size * magnitude * (speed - 0.5 * curvature)
    return phi
```

```python
import functools

import jax
import jax.numpy as jnp
from jax import lax
from jax.experimental import pallas as pl
from jax.experimental.pallas import tpu as pltpu
from jax.sharding import PartitionSpec as P

UPDATES = 2
TAPS = 25
REACH = TAPS // 2
HALO = REACH + 1
SIDE = 16
F32 = jnp.float32
BF16 = jnp.bfloat16
MESH = pl.DeviceIdType.MESH


def split(value):
    high = value.astype(BF16)
    low = (value - high.astype(F32)).astype(BF16)
    return high, low


def toeplitz(offset, keep, taps):
    out = jnp.zeros(offset.shape, F32)
    for k in range(TAPS):
        out = jnp.where(offset == k, taps[k], out)
    if keep is not None:
        out = jnp.where(keep, out, 0.0)
    return out


def divisor(count, limit):
    return max(d for d in range(1, limit + 1) if count % d == 0)


def kernel(
    nx, ny,
    smooth, slope, band, time_step, phi_hbm, sens_hbm,
    out,
    field, part, grad, mag, vel, speed, zmat, ymat,
    send_sem, recv_sem, local_sem,
):
    rows_x, rows_y, depth = out.shape
    ext_x = rows_x + 2 * HALO
    ext_y = rows_y + 2 * SIDE
    out_y = rows_y + 8
    px = lax.axis_index("gx")
    py = lax.axis_index("gy")
    has = {
        "x-": px > 0, "x+": px < nx - 1, "y-": py > 0, "y+": py < ny - 1,
    }
    peer = {
        "x-": (px - 1, py), "x+": (px + 1, py), "y-": (px, py - 1), "y+": (px, py + 1),
    }
    opposite = {"x-": "x+", "x+": "x-", "y-": "y+", "y+": "y-"}
    own_x = pl.ds(HALO, rows_x)
    own_y = pl.ds(SIDE, rows_y)
    low_x, high_x = pl.ds(0, HALO), pl.ds(HALO + rows_x, HALO)
    low_y, high_y = pl.ds(0, SIDE), pl.ds(SIDE + rows_y, SIDE)

    barrier = pltpu.get_barrier_semaphore()
    for side in has:
        @pl.when(has[side])
        def _(side=side):
            pl.semaphore_signal(barrier, inc=1, device_id=peer[side], device_id_type=MESH)

    local = [
        pltpu.make_async_copy(source, field.at[f, own_x, own_y], local_sem.at[f])
        for f, source in enumerate((phi_hbm, sens_hbm))
    ]
    for copy in local:
        copy.start()

    def source_of(f, xs, ys):
        if f == 2:
            return field.at[f, pl.ds(HALO + xs[0], xs[1]), pl.ds(SIDE + ys[0], ys[1])]
        return (phi_hbm, sens_hbm)[f].at[pl.ds(xs[0], xs[1]), pl.ds(ys[0], ys[1])]

    def remote(f, kind):
        sides = ("x+", "x-", "y+", "y-", "y+", "y+", "y-", "y-")
        side = sides[kind]
        if kind == 0:
            src = source_of(f, (rows_x - HALO, HALO), (0, rows_y))
            dst = field.at[f, low_x, own_y]
        elif kind == 1:
            src = source_of(f, (0, HALO), (0, rows_y))
            dst = field.at[f, high_x, own_y]
        elif kind == 2:
            src = source_of(f, (0, rows_x), (rows_y - SIDE, SIDE))
            dst = field.at[f, own_x, low_y]
        elif kind == 3:
            src = source_of(f, (0, rows_x), (0, SIDE))
            dst = field.at[f, own_x, high_y]
        else:
            xs = low_x if kind in (4, 6) else high_x
            ys = pl.ds(rows_y, SIDE) if side == "y+" else pl.ds(SIDE, SIDE)
            src = field.at[f, xs, ys]
            dst = field.at[f, xs, low_y if side == "y+" else high_y]
        copy = pltpu.make_async_remote_copy(
            src_ref=src, dst_ref=dst,
            send_sem=send_sem.at[f, kind], recv_sem=recv_sem.at[f, kind],
            device_id=peer[side], device_id_type=MESH,
        )
        sends, receives = has[side], has[opposite[side]]
        if kind >= 4:
            there = has["x-"] if kind in (4, 6) else has["x+"]
            sends, receives = sends & there, receives & there
        return copy, sends, receives

    def start(f, kinds):
        for kind in kinds:
            copy, sends, _ = remote(f, kind)
            pl.when(sends)(copy.start)

    def arrived(f, kinds):
        for kind in kinds:
            copy, _, receives = remote(f, kind)
            pl.when(receives)(copy.wait_recv)

    def sent(f, kinds):
        for kind in kinds:
            copy, sends, _ = remote(f, kind)
            pl.when(sends)(copy.wait_send)

    neighbours = sum(has[side].astype(jnp.int32) for side in has)
    pl.semaphore_wait(barrier, neighbours)
    start(0, (0, 1, 2, 3))
    start(1, (0, 1, 2, 3))

    for f in range(3):
        @pl.when(px == 0)
        def _(f=f):
            field[f, low_x] = jnp.zeros((HALO, ext_y, depth), F32)

        @pl.when(px == nx - 1)
        def _(f=f):
            field[f, high_x] = jnp.zeros((HALO, ext_y, depth), F32)

        @pl.when(py == 0)
        def _(f=f):
            field[f, :, low_y] = jnp.zeros((ext_x, SIDE, depth), F32)

        @pl.when(py == ny - 1)
        def _(f=f):
            field[f, :, high_y] = jnp.zeros((ext_x, SIDE, depth), F32)

    offset = (
        lax.broadcasted_iota(jnp.int32, (depth, depth), 0)
        - lax.broadcasted_iota(jnp.int32, (depth, depth), 1) + REACH
    )
    for n, taps in enumerate((smooth, slope)):
        high, low = split(toeplitz(offset, None, taps))
        cols = pl.ds(n * depth, depth)
        zmat[pl.ds(0, depth), cols] = high
        zmat[pl.ds(depth, depth), cols] = high
        zmat[pl.ds(2 * depth, depth), cols] = low
    row = lax.broadcasted_iota(jnp.int32, (out_y, ext_y), 0)
    cell = jnp.where(row == out_y - 1, -1, row)
    keep = (cell <= rows_y) & ((cell >= 0) | (py > 0)) & ((cell < rows_y) | (py < ny - 1))
    offset = lax.broadcasted_iota(jnp.int32, (out_y, ext_y), 1) - cell - (SIDE - REACH)
    pieces = []
    for taps in (smooth, slope):
        high, low = split(toeplitz(offset, keep, taps))
        pieces.append(jnp.concatenate([high.astype(F32), high.astype(F32), low.astype(F32)], axis=1))
    ymat[...] = jnp.concatenate(pieces, axis=0).astype(BF16)

    def planes(f, rows):
        for r in rows:
            high, low = split(field[f, r])
            lhs = jnp.concatenate([high, low, high], axis=1)
            if f == 1:
                z_out = jnp.dot(lhs, zmat[:, :depth], preferred_element_type=F32)
            else:
                z_out = jnp.dot(lhs, zmat[...], preferred_element_type=F32)
            high, low = split(z_out)
            rhs = jnp.concatenate([high, low, high], axis=0)
            if f == 1:
                part[3, r] = jnp.dot(ymat[:out_y], rhs, preferred_element_type=F32)
            else:
                y_out = jnp.dot(ymat[...], rhs, preferred_element_type=F32)
                part[0, r] = y_out[:out_y, :depth]
                part[1, r] = y_out[out_y:, :depth]
                part[2, r] = y_out[:out_y, depth:]

    def own_planes(f):
        step = divisor(rows_x, 8)

        def body(i, carry):
            planes(f, [HALO + i * step + r for r in range(step)])
            return carry

        lax.fori_loop(0, rows_x // step, body, 0)

    def halo_planes(f):
        def body(i, carry):
            planes(f, [i, HALO + rows_x + i])
            return carry

        lax.fori_loop(0, HALO, body, 0)

    group = divisor(rows_x + 2, 17)
    tiles = out_y // 8
    steps = tiles * ((rows_x + 2) // group)

    def smooth_x(n, first, rows):
        acc = [None] * group
        for j in range(group + TAPS - 1):
            value = part[n, first + j, rows]
            for g in range(max(0, j - TAPS + 1), min(group, j + 1)):
                term = smooth[j - g] * value
                acc[g] = term if acc[g] is None else acc[g] + term
        return acc

    def slope_x(n, first, rows):
        values = [part[n, first + j, rows] for j in range(group + TAPS - 1)]
        acc = []
        for g in range(group):
            total = None
            for k in range(REACH):
                term = slope[REACH + 1 + k] * (values[g + REACH + 1 + k] - values[g + REACH - 1 - k])
                total = term if total is None else total + term
            acc.append(total)
        return acc

    def place(i):
        return (i // tiles) * group, pl.ds(pl.multiple_of((i % tiles) * 8, 8), 8)

    def normals():
        def body(i, carry):
            first, rows = place(i)
            for g, value in enumerate(slope_x(0, first, rows)):
                grad[0, first + g, rows] = value
            for g, value in enumerate(smooth_x(1, first, rows)):
                grad[1, first + g, rows] = value
            for g, gz in enumerate(smooth_x(2, first, rows)):
                gx = grad[0, first + g, rows]
                gy = grad[1, first + g, rows]
                square = gx * gx + gy * gy + gz * gz + 1.0
                inverse = lax.rsqrt(square)
                grad[0, first + g, rows] = gx * inverse
                grad[1, first + g, rows] = gy * inverse
                grad[2, first + g, rows] = gz * inverse
                mag[first + g, rows] = square * inverse
            return carry

        lax.fori_loop(0, steps, body, 0)
        for edge, at in ((px == 0, 0), (px == nx - 1, rows_x + 1)):
            @pl.when(edge)
            def _(at=at):
                grad[0, at] = jnp.zeros((out_y, depth), F32)

    def velocity():
        def body(i, carry):
            first, rows = place(i)
            for g, value in enumerate(smooth_x(3, first, rows)):
                vel[first + g, rows] = value
            return carry

        lax.fori_loop(0, steps, body, 0)
        for edge, at in ((px == 0, 0), (px == nx - 1, rows_x + 1)):
            @pl.when(edge)
            def _(at=at):
                vel[at] = jnp.zeros((out_y, depth), F32)

    lane = lax.broadcasted_iota(jnp.int32, (rows_y, depth), 1)

    def around_y(value):
        after = pltpu.roll(value, out_y - 1, 0)[:rows_y]
        before = pltpu.roll(value, 1, 0)[:rows_y]
        return after, before

    def around_z(value):
        after = jnp.where(lane == depth - 1, 0.0, pltpu.roll(value, depth - 1, 1))
        before = jnp.where(lane == 0, 0.0, pltpu.roll(value, 1, 1))
        return after, before

    def speeds():
        def body(x, carry):
            value = vel[x + 1]
            after_y, before_y = around_y(value)
            inner = value[:rows_y]
            after_z, before_z = around_z(inner)
            total = inner + vel[x + 2, :rows_y] + vel[x, :rows_y]
            total = total + after_y + before_y + after_z + before_z
            speed[x] = total * (1.0 / 7.0)
            return carry

        lax.fori_loop(0, rows_x, body, 0)

    blocks_x, blocks_y, blocks_z = band.shape
    wide_x, wide_y, wide_z = rows_x // blocks_x, rows_y // blocks_y, depth // blocks_z
    lane_row = lax.broadcasted_iota(jnp.int32, (wide_y, depth), 1)

    def advance(f, store):
        for p in range(blocks_x):
            strips = []
            for q in range(blocks_y):
                strip = jnp.zeros((wide_y, depth), F32)
                for r in range(blocks_z):
                    entry = band[p, q, r].astype(F32) * time_step[0]
                    strip = jnp.where((lane_row >= r * wide_z) & (lane_row < (r + 1) * wide_z), entry, strip)
                strips.append(strip)
            step_size = jnp.concatenate(strips, axis=0)

            def body(i, carry):
                x = p * wide_x + i
                after_y, before_y = around_y(grad[1, x + 1])
                after_z, before_z = around_z(grad[2, x + 1, :rows_y])
                curvature = 0.5 * (
                    (grad[0, x + 2, :rows_y] - grad[0, x, :rows_y])
                    + (after_y - before_y) + (after_z - before_z)
                )
                phi = field[f, HALO + x, own_y]
                store(x, phi - step_size * mag[x + 1, :rows_y] * (speed[x] - 0.5 * curvature))
                return carry

            lax.fori_loop(0, wide_x, body, 0)

    def store_next(x, value):
        field[2, HALO + x, own_y] = value

    def store_out(x, value):
        out[x] = value

    local[0].wait()
    arrived(0, (2, 3))
    own_planes(0)
    local[1].wait()
    arrived(0, (0, 1))
    start(0, (4, 5, 6, 7))
    arrived(1, (2, 3))
    own_planes(1)
    arrived(0, (4, 5, 6, 7))
    halo_planes(0)
    normals()
    arrived(1, (0, 1))
    start(1, (4, 5, 6, 7))
    arrived(1, (4, 5, 6, 7))
    halo_planes(1)
    velocity()
    speeds()
    advance(0, store_next)
    start(2, (0, 1, 2, 3))
    arrived(2, (2, 3))
    own_planes(2)
    arrived(2, (0, 1))
    start(2, (4, 5, 6, 7))
    arrived(2, (4, 5, 6, 7))
    halo_planes(2)
    normals()
    advance(2, store_out)
    for f in range(3):
        sent(f, range(8))


def per_device(nx, ny, level_set, sensitivity, smooth_taps, slope_taps, band, time_step):
    rows_x, rows_y, depth = level_set.shape
    ext_x = rows_x + 2 * HALO
    ext_y = rows_y + 2 * SIDE
    out_y = rows_y + 8
    smem = pl.BlockSpec(memory_space=pltpu.SMEM)
    hbm = pl.BlockSpec(memory_space=pl.ANY)
    return pl.pallas_call(
        functools.partial(kernel, nx, ny),
        out_shape=jax.ShapeDtypeStruct(level_set.shape, F32),
        in_specs=[smem, smem, smem, smem, hbm, hbm],
        out_specs=pl.BlockSpec(memory_space=pltpu.VMEM),
        scratch_shapes=[
            pltpu.VMEM((3, ext_x, ext_y, depth), F32),
            pltpu.VMEM((4, ext_x, out_y, depth), F32),
            pltpu.VMEM((3, rows_x + 2, out_y, depth), F32),
            pltpu.VMEM((rows_x + 2, out_y, depth), F32),
            pltpu.VMEM((rows_x + 2, out_y, depth), F32),
            pltpu.VMEM((rows_x, rows_y, depth), F32),
            pltpu.VMEM((3 * depth, 2 * depth), BF16),
            pltpu.VMEM((2 * out_y, 3 * ext_y), BF16),
            pltpu.SemaphoreType.DMA((3, 8)),
            pltpu.SemaphoreType.DMA((3, 8)),
            pltpu.SemaphoreType.DMA((2,)),
        ],
        compiler_params=pltpu.CompilerParams(
            collective_id=0, has_side_effects=True, vmem_limit_bytes=40 * 1024 * 1024,
        ),
        name="level_set_updates",
    )(smooth_taps, slope_taps, band, time_step, level_set, sensitivity)


def solution(mesh):
    return jax.shard_map(
        functools.partial(per_device, mesh.shape["gx"], mesh.shape["gy"]),
        mesh=mesh,
        in_specs=(P("gx", "gy", None), P("gx", "gy", None), P(), P(), P("gx", "gy", None), P()),
        out_specs=P("gx", "gy", None),
        check_vma=False,
    )
```

```python
import functools

import jax
import jax.numpy as jnp
from jax import lax
from jax.experimental import pallas as pl
from jax.experimental.pallas import tpu as pltpu
from jax.sharding import PartitionSpec as P

UPDATES = 2
TAPS = 25
REACH = TAPS // 2
HALO = REACH + 1
SIDE = 16
F32 = jnp.float32
BF16 = jnp.bfloat16
MESH = pl.DeviceIdType.MESH


def split(value):
    high = value.astype(BF16)
    low = (value - high.astype(F32)).astype(BF16)
    return high, low


def toeplitz(offset, keep, taps):
    out = jnp.zeros(offset.shape, F32)
    for k in range(TAPS):
        out = jnp.where(offset == k, taps[k], out)
    if keep is not None:
        out = jnp.where(keep, out, 0.0)
    return out


def divisor(count, limit):
    return max(d for d in range(1, limit + 1) if count % d == 0)


def kernel(
    nx, ny,
    smooth, slope, band, time_step, phi_hbm, sens_hbm,
    out,
    field, part, grad, mag, vel, speed, zmat, ymat,
    send_sem, recv_sem, local_sem,
):
    rows_x, rows_y, depth = out.shape
    ext_x = rows_x + 2 * HALO
    ext_y = rows_y + 2 * SIDE
    out_y = rows_y + 8
    px = lax.axis_index("gx")
    py = lax.axis_index("gy")
    has = {
        "x-": px > 0, "x+": px < nx - 1, "y-": py > 0, "y+": py < ny - 1,
    }
    peer = {
        "x-": (px - 1, py), "x+": (px + 1, py), "y-": (px, py - 1), "y+": (px, py + 1),
    }
    opposite = {"x-": "x+", "x+": "x-", "y-": "y+", "y+": "y-"}
    own_x = pl.ds(HALO, rows_x)
    own_y = pl.ds(SIDE, rows_y)
    low_x, high_x = pl.ds(0, HALO), pl.ds(HALO + rows_x, HALO)
    low_y, high_y = pl.ds(0, SIDE), pl.ds(SIDE + rows_y, SIDE)

    barrier = pltpu.get_barrier_semaphore()
    for side in has:
        @pl.when(has[side])
        def _(side=side):
            pl.semaphore_signal(barrier, inc=1, device_id=peer[side], device_id_type=MESH)

    local = [
        pltpu.make_async_copy(source, field.at[f, own_x, own_y], local_sem.at[f])
        for f, source in enumerate((phi_hbm, sens_hbm))
    ]
    for copy in local:
        copy.start()

    def source_of(f, xs, ys):
        if f == 2:
            return field.at[f, pl.ds(HALO + xs[0], xs[1]), pl.ds(SIDE + ys[0], ys[1])]
        return (phi_hbm, sens_hbm)[f].at[pl.ds(xs[0], xs[1]), pl.ds(ys[0], ys[1])]

    def remote(f, kind):
        sides = ("x+", "x-", "y+", "y-", "y+", "y+", "y-", "y-")
        side = sides[kind]
        if kind == 0:
            src = source_of(f, (rows_x - HALO, HALO), (0, rows_y))
            dst = field.at[f, low_x, own_y]
        elif kind == 1:
            src = source_of(f, (0, HALO), (0, rows_y))
            dst = field.at[f, high_x, own_y]
        elif kind == 2:
            src = source_of(f, (0, rows_x), (rows_y - SIDE, SIDE))
            dst = field.at[f, own_x, low_y]
        elif kind == 3:
            src = source_of(f, (0, rows_x), (0, SIDE))
            dst = field.at[f, own_x, high_y]
        else:
            xs = low_x if kind in (4, 6) else high_x
            ys = pl.ds(rows_y, SIDE) if side == "y+" else pl.ds(SIDE, SIDE)
            src = field.at[f, xs, ys]
            dst = field.at[f, xs, low_y if side == "y+" else high_y]
        copy = pltpu.make_async_remote_copy(
            src_ref=src, dst_ref=dst,
            send_sem=send_sem.at[f, kind], recv_sem=recv_sem.at[f, kind],
            device_id=peer[side], device_id_type=MESH,
        )
        sends, receives = has[side], has[opposite[side]]
        if kind >= 4:
            there = has["x-"] if kind in (4, 6) else has["x+"]
            sends, receives = sends & there, receives & there
        return copy, sends, receives

    def start(f, kinds):
        for kind in kinds:
            copy, sends, _ = remote(f, kind)
            pl.when(sends)(copy.start)

    def arrived(f, kinds):
        for kind in kinds:
            copy, _, receives = remote(f, kind)
            pl.when(receives)(copy.wait_recv)

    def sent(f, kinds):
        for kind in kinds:
            copy, sends, _ = remote(f, kind)
            pl.when(sends)(copy.wait_send)

    neighbours = sum(has[side].astype(jnp.int32) for side in has)
    pl.semaphore_wait(barrier, neighbours)
    start(0, (0, 1, 2, 3))
    start(1, (0, 1, 2, 3))

    for f in range(3):
        @pl.when(px == 0)
        def _(f=f):
            field[f, low_x] = jnp.zeros((HALO, ext_y, depth), F32)

        @pl.when(px == nx - 1)
        def _(f=f):
            field[f, high_x] = jnp.zeros((HALO, ext_y, depth), F32)

        @pl.when(py == 0)
        def _(f=f):
            field[f, :, low_y] = jnp.zeros((ext_x, SIDE, depth), F32)

        @pl.when(py == ny - 1)
        def _(f=f):
            field[f, :, high_y] = jnp.zeros((ext_x, SIDE, depth), F32)

    offset = (
        lax.broadcasted_iota(jnp.int32, (depth, depth), 0)
        - lax.broadcasted_iota(jnp.int32, (depth, depth), 1) + REACH
    )
    for n, taps in enumerate((smooth, slope)):
        high, low = split(toeplitz(offset, None, taps))
        cols = pl.ds(n * depth, depth)
        zmat[pl.ds(0, depth), cols] = high
        zmat[pl.ds(depth, depth), cols] = high
        zmat[pl.ds(2 * depth, depth), cols] = low
    row = lax.broadcasted_iota(jnp.int32, (out_y, ext_y), 0)
    cell = jnp.where(row == out_y - 1, -1, row)
    keep = (cell <= rows_y) & ((cell >= 0) | (py > 0)) & ((cell < rows_y) | (py < ny - 1))
    offset = lax.broadcasted_iota(jnp.int32, (out_y, ext_y), 1) - cell - (SIDE - REACH)
    pieces = []
    for taps in (smooth, slope):
        high, low = split(toeplitz(offset, keep, taps))
        pieces.append(jnp.concatenate([high.astype(F32), high.astype(F32), low.astype(F32)], axis=1))
    ymat[...] = jnp.concatenate(pieces, axis=0).astype(BF16)

    def planes(f, first, count):
        high, low = split(field[f, pl.ds(first, count)].reshape(count * ext_y, depth))
        lhs = jnp.concatenate([high, low, high], axis=1)
        width = depth if f == 1 else 2 * depth
        high, low = split(jnp.dot(lhs, zmat[:, :width], preferred_element_type=F32))

        def stack(r):
            rows = slice(r * ext_y, (r + 1) * ext_y)
            return jnp.concatenate([high[rows], low[rows], high[rows]], axis=0)

        if f == 1:
            for r in range(0, count, 2):
                both = [stack(q) for q in range(r, min(r + 2, count))]
                y_out = jnp.dot(ymat[:out_y], jnp.concatenate(both, axis=1), preferred_element_type=F32)
                for q in range(len(both)):
                    part[3, first + r + q] = y_out[:, q * depth:(q + 1) * depth]
        else:
            for r in range(count):
                y_out = jnp.dot(ymat[...], stack(r), preferred_element_type=F32)
                part[0, first + r] = y_out[:out_y, :depth]
                part[1, first + r] = y_out[out_y:, :depth]
                part[2, first + r] = y_out[:out_y, depth:]

    def own_planes(f):
        step = divisor(rows_x, 16)

        def body(i, carry):
            planes(f, HALO + i * step, step)
            return carry

        lax.fori_loop(0, rows_x // step, body, 0)

    def halo_planes(f):
        def body(i, carry):
            planes(f, i * (HALO + rows_x), HALO)
            return carry

        lax.fori_loop(0, 2, body, 0)

    group = divisor(rows_x + 2, 17)
    tiles = out_y // 8
    steps = tiles * ((rows_x + 2) // group)

    def smooth_x(n, first, rows):
        acc = [None] * group
        for j in range(group + TAPS - 1):
            value = part[n, first + j, rows]
            for g in range(max(0, j - TAPS + 1), min(group, j + 1)):
                term = smooth[j - g] * value
                acc[g] = term if acc[g] is None else acc[g] + term
        return acc

    def slope_x(n, first, rows):
        values = [part[n, first + j, rows] for j in range(group + TAPS - 1)]
        acc = []
        for g in range(group):
            total = None
            for k in range(REACH):
                term = slope[REACH + 1 + k] * (values[g + REACH + 1 + k] - values[g + REACH - 1 - k])
                total = term if total is None else total + term
            acc.append(total)
        return acc

    def place(i):
        return (i // tiles) * group, pl.ds(pl.multiple_of((i % tiles) * 8, 8), 8)

    def normals():
        def body(i, carry):
            first, rows = place(i)
            for g, value in enumerate(slope_x(0, first, rows)):
                grad[0, first + g, rows] = value
            for g, value in enumerate(smooth_x(1, first, rows)):
                grad[1, first + g, rows] = value
            for g, gz in enumerate(smooth_x(2, first, rows)):
                gx = grad[0, first + g, rows]
                gy = grad[1, first + g, rows]
                square = gx * gx + gy * gy + gz * gz + 1.0
                inverse = lax.rsqrt(square)
                grad[0, first + g, rows] = gx * inverse
                grad[1, first + g, rows] = gy * inverse
                grad[2, first + g, rows] = gz * inverse
                mag[first + g, rows] = square * inverse
            return carry

        lax.fori_loop(0, steps, body, 0)
        for edge, at in ((px == 0, 0), (px == nx - 1, rows_x + 1)):
            @pl.when(edge)
            def _(at=at):
                grad[0, at] = jnp.zeros((out_y, depth), F32)

    def velocity():
        def body(i, carry):
            first, rows = place(i)
            for g, value in enumerate(smooth_x(3, first, rows)):
                vel[first + g, rows] = value
            return carry

        lax.fori_loop(0, steps, body, 0)
        for edge, at in ((px == 0, 0), (px == nx - 1, rows_x + 1)):
            @pl.when(edge)
            def _(at=at):
                vel[at] = jnp.zeros((out_y, depth), F32)

    lane = lax.broadcasted_iota(jnp.int32, (rows_y, depth), 1)

    def around_y(value):
        after = pltpu.roll(value, out_y - 1, 0)[:rows_y]
        before = pltpu.roll(value, 1, 0)[:rows_y]
        return after, before

    def around_z(value):
        after = jnp.where(lane == depth - 1, 0.0, pltpu.roll(value, depth - 1, 1))
        before = jnp.where(lane == 0, 0.0, pltpu.roll(value, 1, 1))
        return after, before

    def speeds():
        step = divisor(rows_x, 4)

        def body(i, carry):
            for u in range(step):
                x = i * step + u
                value = vel[x + 1]
                after_y, before_y = around_y(value)
                inner = value[:rows_y]
                after_z, before_z = around_z(inner)
                total = inner + vel[x + 2, :rows_y] + vel[x, :rows_y]
                total = total + after_y + before_y + after_z + before_z
                speed[x] = total * (1.0 / 7.0)
            return carry

        lax.fori_loop(0, rows_x // step, body, 0)

    blocks_x, blocks_y, blocks_z = band.shape
    wide_x, wide_y, wide_z = rows_x // blocks_x, rows_y // blocks_y, depth // blocks_z
    lane_row = lax.broadcasted_iota(jnp.int32, (wide_y, depth), 1)

    def advance(f, store):
        for p in range(blocks_x):
            strips = []
            for q in range(blocks_y):
                strip = jnp.zeros((wide_y, depth), F32)
                for r in range(blocks_z):
                    entry = band[p, q, r].astype(F32) * time_step[0]
                    strip = jnp.where((lane_row >= r * wide_z) & (lane_row < (r + 1) * wide_z), entry, strip)
                strips.append(strip)
            step_size = jnp.concatenate(strips, axis=0)

            step = divisor(wide_x, 4)

            def body(i, carry):
                for u in range(step):
                    x = p * wide_x + i * step + u
                    after_y, before_y = around_y(grad[1, x + 1])
                    after_z, before_z = around_z(grad[2, x + 1, :rows_y])
                    curvature = 0.5 * (
                        (grad[0, x + 2, :rows_y] - grad[0, x, :rows_y])
                        + (after_y - before_y) + (after_z - before_z)
                    )
                    phi = field[f, HALO + x, own_y]
                    store(x, phi - step_size * mag[x + 1, :rows_y] * (speed[x] - 0.5 * curvature))
                return carry

            lax.fori_loop(0, wide_x // step, body, 0)

    def store_next(x, value):
        field[2, HALO + x, own_y] = value

    def store_out(x, value):
        out[x] = value

    local[0].wait()
    arrived(0, (2, 3))
    own_planes(0)
    local[1].wait()
    arrived(0, (0, 1))
    start(0, (4, 5, 6, 7))
    arrived(1, (2, 3))
    own_planes(1)
    arrived(0, (4, 5, 6, 7))
    halo_planes(0)
    normals()
    arrived(1, (0, 1))
    start(1, (4, 5, 6, 7))
    arrived(1, (4, 5, 6, 7))
    halo_planes(1)
    velocity()
    speeds()
    advance(0, store_next)
    start(2, (0, 1, 2, 3))
    arrived(2, (2, 3))
    own_planes(2)
    arrived(2, (0, 1))
    start(2, (4, 5, 6, 7))
    arrived(2, (4, 5, 6, 7))
    halo_planes(2)
    normals()
    advance(2, store_out)
    for f in range(3):
        sent(f, range(8))


def per_device(nx, ny, level_set, sensitivity, smooth_taps, slope_taps, band, time_step):
    rows_x, rows_y, depth = level_set.shape
    ext_x = rows_x + 2 * HALO
    ext_y = rows_y + 2 * SIDE
    out_y = rows_y + 8
    smem = pl.BlockSpec(memory_space=pltpu.SMEM)
    hbm = pl.BlockSpec(memory_space=pl.ANY)
    return pl.pallas_call(
        functools.partial(kernel, nx, ny),
        out_shape=jax.ShapeDtypeStruct(level_set.shape, F32),
        in_specs=[smem, smem, smem, smem, hbm, hbm],
        out_specs=pl.BlockSpec(memory_space=pltpu.VMEM),
        scratch_shapes=[
            pltpu.VMEM((3, ext_x, ext_y, depth), F32),
            pltpu.VMEM((4, ext_x, out_y, depth), F32),
            pltpu.VMEM((3, rows_x + 2, out_y, depth), F32),
            pltpu.VMEM((rows_x + 2, out_y, depth), F32),
            pltpu.VMEM((rows_x + 2, out_y, depth), F32),
            pltpu.VMEM((rows_x, rows_y, depth), F32),
            pltpu.VMEM((3 * depth, 2 * depth), BF16),
            pltpu.VMEM((2 * out_y, 3 * ext_y), BF16),
            pltpu.SemaphoreType.DMA((3, 8)),
            pltpu.SemaphoreType.DMA((3, 8)),
            pltpu.SemaphoreType.DMA((2,)),
        ],
        compiler_params=pltpu.CompilerParams(
            collective_id=0, has_side_effects=True, vmem_limit_bytes=40 * 1024 * 1024,
        ),
        name="level_set_updates",
    )(smooth_taps, slope_taps, band, time_step, level_set, sensitivity)


def solution(mesh):
    return jax.shard_map(
        functools.partial(per_device, mesh.shape["gx"], mesh.shape["gy"]),
        mesh=mesh,
        in_specs=(P("gx", "gy", None), P("gx", "gy", None), P(), P(), P("gx", "gy", None), P()),
        out_specs=P("gx", "gy", None),
        check_vma=False,
    )
```

```python
import functools

import jax
import jax.numpy as jnp
from jax import lax
from jax.experimental import pallas as pl
from jax.experimental.pallas import tpu as pltpu
from jax.sharding import PartitionSpec as P

UPDATES = 2
TAPS = 25
REACH = TAPS // 2
HALO = REACH + 1
SIDE = 16
F32 = jnp.float32
BF16 = jnp.bfloat16
MESH = pl.DeviceIdType.MESH


def split(value):
    high = value.astype(BF16)
    low = (value - high.astype(F32)).astype(BF16)
    return high, low


def toeplitz(offset, keep, taps):
    out = jnp.zeros(offset.shape, F32)
    for k in range(TAPS):
        out = jnp.where(offset == k, taps[k], out)
    if keep is not None:
        out = jnp.where(keep, out, 0.0)
    return out


def divisor(count, limit):
    return max(d for d in range(1, limit + 1) if count % d == 0)


def kernel(
    nx, ny,
    smooth, slope, band, time_step, phi_hbm, sens_hbm,
    out,
    field, part, grad, mag, vel, speed, zmat, ymat,
    send_sem, recv_sem, local_sem,
):
    rows_x, rows_y, depth = out.shape
    ext_x = rows_x + 2 * HALO
    ext_y = rows_y + 2 * SIDE
    out_y = rows_y + 8
    px = lax.axis_index("gx")
    py = lax.axis_index("gy")
    has = {
        "x-": px > 0, "x+": px < nx - 1, "y-": py > 0, "y+": py < ny - 1,
    }
    peer = {
        "x-": (px - 1, py), "x+": (px + 1, py), "y-": (px, py - 1), "y+": (px, py + 1),
    }
    opposite = {"x-": "x+", "x+": "x-", "y-": "y+", "y+": "y-"}
    own_x = pl.ds(HALO, rows_x)
    own_y = pl.ds(SIDE, rows_y)
    low_x, high_x = pl.ds(0, HALO), pl.ds(HALO + rows_x, HALO)
    low_y, high_y = pl.ds(0, SIDE), pl.ds(SIDE + rows_y, SIDE)

    barrier = pltpu.get_barrier_semaphore()
    for side in has:
        @pl.when(has[side])
        def _(side=side):
            pl.semaphore_signal(barrier, inc=1, device_id=peer[side], device_id_type=MESH)

    local = [
        pltpu.make_async_copy(source, field.at[f, own_x, own_y], local_sem.at[f])
        for f, source in enumerate((phi_hbm, sens_hbm))
    ]
    for copy in local:
        copy.start()

    def source_of(f, xs, ys):
        if f == 2:
            return field.at[f, pl.ds(HALO + xs[0], xs[1]), pl.ds(SIDE + ys[0], ys[1])]
        return (phi_hbm, sens_hbm)[f].at[pl.ds(xs[0], xs[1]), pl.ds(ys[0], ys[1])]

    cut = HALO - HALO // 2
    pieces = ((0, cut), (cut, HALO - cut))
    first_x = {"x-": 0, "x+": HALO + rows_x}
    mains = (0, 1)
    edges = tuple((2 + 6 * n, 3 + 6 * n) for n in range(2))
    corners = tuple(tuple(range(4 + 6 * n, 8 + 6 * n)) for n in range(2))

    def remote(f, kind):
        there = None
        if kind in mains:
            side = ("y+", "y-")[kind]
            ys = (rows_y - SIDE, SIDE) if side == "y+" else (0, SIDE)
            src = source_of(f, (0, rows_x), ys)
            dst = field.at[f, own_x, low_y if side == "y+" else high_y]
        else:
            at, size = pieces[(kind - 2) // 6]
            which = (kind - 2) % 6
            if which < 2:
                side = ("x+", "x-")[which]
                begin = rows_x - HALO + at if side == "x+" else at
                src = source_of(f, (begin, size), (0, rows_y))
                dst = field.at[f, pl.ds(first_x[opposite[side]] + at, size), own_y]
            else:
                side = ("y+", "y-")[(which - 2) // 2]
                there = ("x-", "x+")[(which - 2) % 2]
                xs = pl.ds(first_x[there] + at, size)
                src = field.at[f, xs, pl.ds(rows_y if side == "y+" else SIDE, SIDE)]
                dst = field.at[f, xs, low_y if side == "y+" else high_y]
        copy = pltpu.make_async_remote_copy(
            src_ref=src, dst_ref=dst,
            send_sem=send_sem.at[f, kind], recv_sem=recv_sem.at[f, kind],
            device_id=peer[side], device_id_type=MESH,
        )
        sends, receives = has[side], has[opposite[side]]
        if there is not None:
            sends, receives = sends & has[there], receives & has[there]
        return copy, sends, receives

    def start(f, kinds):
        for kind in kinds:
            copy, sends, _ = remote(f, kind)
            pl.when(sends)(copy.start)

    def arrived(f, kinds):
        for kind in kinds:
            copy, _, receives = remote(f, kind)
            pl.when(receives)(copy.wait_recv)

    def sent(f, kinds):
        for kind in kinds:
            copy, sends, _ = remote(f, kind)
            pl.when(sends)(copy.wait_send)

    neighbours = sum(has[side].astype(jnp.int32) for side in has)
    pl.semaphore_wait(barrier, neighbours)
    for f in range(2):
        start(f, edges[0] + mains + edges[1])

    for f in range(3):
        @pl.when(px == 0)
        def _(f=f):
            field[f, low_x] = jnp.zeros((HALO, ext_y, depth), F32)

        @pl.when(px == nx - 1)
        def _(f=f):
            field[f, high_x] = jnp.zeros((HALO, ext_y, depth), F32)

        @pl.when(py == 0)
        def _(f=f):
            field[f, :, low_y] = jnp.zeros((ext_x, SIDE, depth), F32)

        @pl.when(py == ny - 1)
        def _(f=f):
            field[f, :, high_y] = jnp.zeros((ext_x, SIDE, depth), F32)

    offset = (
        lax.broadcasted_iota(jnp.int32, (depth, depth), 0)
        - lax.broadcasted_iota(jnp.int32, (depth, depth), 1) + REACH
    )
    for n, taps in enumerate((smooth, slope)):
        high, low = split(toeplitz(offset, None, taps))
        cols = pl.ds(n * depth, depth)
        zmat[pl.ds(0, depth), cols] = high
        zmat[pl.ds(depth, depth), cols] = high
        zmat[pl.ds(2 * depth, depth), cols] = low
    row = lax.broadcasted_iota(jnp.int32, (out_y, ext_y), 0)
    cell = jnp.where(row == out_y - 1, -1, row)
    keep = (cell <= rows_y) & ((cell >= 0) | (py > 0)) & ((cell < rows_y) | (py < ny - 1))
    offset = lax.broadcasted_iota(jnp.int32, (out_y, ext_y), 1) - cell - (SIDE - REACH)
    strips = []
    for taps in (smooth, slope):
        high, low = split(toeplitz(offset, keep, taps))
        strips.append(jnp.concatenate([high.astype(F32), high.astype(F32), low.astype(F32)], axis=1))
    ymat[...] = jnp.concatenate(strips, axis=0).astype(BF16)

    def planes(f, first, count):
        high, low = split(field[f, pl.ds(first, count)].reshape(count * ext_y, depth))
        lhs = jnp.concatenate([high, low, high], axis=1)
        width = depth if f == 1 else 2 * depth
        high, low = split(jnp.dot(lhs, zmat[:, :width], preferred_element_type=F32))

        def stack(r):
            rows = slice(r * ext_y, (r + 1) * ext_y)
            return jnp.concatenate([high[rows], low[rows], high[rows]], axis=0)

        if f == 1:
            for r in range(0, count, 2):
                both = [stack(q) for q in range(r, min(r + 2, count))]
                y_out = jnp.dot(ymat[:out_y], jnp.concatenate(both, axis=1), preferred_element_type=F32)
                for q in range(len(both)):
                    part[3, first + r + q] = y_out[:, q * depth:(q + 1) * depth]
        else:
            for r in range(count):
                y_out = jnp.dot(ymat[...], stack(r), preferred_element_type=F32)
                part[0, first + r] = y_out[:out_y, :depth]
                part[1, first + r] = y_out[out_y:, :depth]
                part[2, first + r] = y_out[:out_y, depth:]

    def own_planes(f):
        step = divisor(rows_x, 16)

        def body(i, carry):
            planes(f, HALO + i * step, step)
            return carry

        lax.fori_loop(0, rows_x // step, body, 0)

    def halo_planes(f, n):
        at, size = pieces[n]

        def body(i, carry):
            planes(f, i * (HALO + rows_x) + at, size)
            return carry

        lax.fori_loop(0, 2, body, 0)

    group = divisor(rows_x + 2, 17)
    tiles = out_y // 8

    def is_own(row):
        return HALO <= row < HALO + rows_x

    def smooth_x(n, first, rows, own, target):
        acc = [None] * group
        for j in range(group + TAPS - 1):
            if is_own(first + j) != own:
                continue
            value = part[n, first + j, rows]
            for g in range(max(0, j - TAPS + 1), min(group, j + 1)):
                term = smooth[j - g] * value
                acc[g] = term if acc[g] is None else acc[g] + term
        return finish(acc, first, rows, own, target)

    def finish(acc, first, rows, own, target):
        if own:
            for g in range(group):
                target(first + g, rows, acc[g])
            return None
        return acc

    def slope_x(n, first, rows, own, target):
        values = {
            j: part[n, first + j, rows]
            for j in range(group + TAPS - 1) if is_own(first + j) == own
        }
        acc = []
        for g in range(group):
            total = None
            for k in range(REACH + 1, TAPS):
                after, before = values.get(g + k), values.get(g + TAPS - 1 - k)
                if after is None and before is None:
                    continue
                if before is None:
                    pair = after
                elif after is None:
                    pair = -before
                else:
                    pair = after - before
                term = slope[k] * pair
                total = term if total is None else total + term
            acc.append(total)
        return finish(acc, first, rows, own, target)

    def each_tile(work):
        for first in range(0, rows_x + 2, group):
            def body(i, carry, first=first):
                work(first, pl.ds(pl.multiple_of(i * 8, 8), 8))
                return carry

            lax.fori_loop(0, tiles, body, 0)

    def plus(ref_value, extra):
        return ref_value if extra is None else ref_value + extra

    def put_grad(n):
        def target(x, rows, value):
            grad[n, x, rows] = jnp.zeros((8, depth), F32) if value is None else value
        return target

    def put_vel(x, rows, value):
        vel[x, rows] = jnp.zeros((8, depth), F32) if value is None else value

    def own_gradients():
        def work(first, rows):
            slope_x(0, first, rows, True, put_grad(0))
            smooth_x(1, first, rows, True, put_grad(1))
            smooth_x(2, first, rows, True, put_grad(2))

        each_tile(work)

    def normals():
        def work(first, rows):
            more_x = slope_x(0, first, rows, False, None)
            more_y = smooth_x(1, first, rows, False, None)
            more_z = smooth_x(2, first, rows, False, None)
            for g in range(group):
                gx = plus(grad[0, first + g, rows], more_x[g])
                gy = plus(grad[1, first + g, rows], more_y[g])
                gz = plus(grad[2, first + g, rows], more_z[g])
                square = gx * gx + gy * gy + gz * gz + 1.0
                inverse = lax.rsqrt(square)
                grad[0, first + g, rows] = gx * inverse
                grad[1, first + g, rows] = gy * inverse
                grad[2, first + g, rows] = gz * inverse
                mag[first + g, rows] = square * inverse

        each_tile(work)
        for edge, at in ((px == 0, 0), (px == nx - 1, rows_x + 1)):
            @pl.when(edge)
            def _(at=at):
                grad[0, at] = jnp.zeros((out_y, depth), F32)

    def own_velocity():
        each_tile(lambda first, rows: smooth_x(3, first, rows, True, put_vel))

    def velocity():
        def work(first, rows):
            for g, extra in enumerate(smooth_x(3, first, rows, False, None)):
                if extra is not None:
                    vel[first + g, rows] = vel[first + g, rows] + extra

        each_tile(work)
        for edge, at in ((px == 0, 0), (px == nx - 1, rows_x + 1)):
            @pl.when(edge)
            def _(at=at):
                vel[at] = jnp.zeros((out_y, depth), F32)

    lane = lax.broadcasted_iota(jnp.int32, (rows_y, depth), 1)

    def around_y(value):
        after = pltpu.roll(value, out_y - 1, 0)[:rows_y]
        before = pltpu.roll(value, 1, 0)[:rows_y]
        return after, before

    def around_z(value):
        after = jnp.where(lane == depth - 1, 0.0, pltpu.roll(value, depth - 1, 1))
        before = jnp.where(lane == 0, 0.0, pltpu.roll(value, 1, 1))
        return after, before

    def speeds():
        step = divisor(rows_x, 4)

        def body(i, carry):
            for u in range(step):
                x = i * step + u
                value = vel[x + 1]
                after_y, before_y = around_y(value)
                inner = value[:rows_y]
                after_z, before_z = around_z(inner)
                total = inner + vel[x + 2, :rows_y] + vel[x, :rows_y]
                total = total + after_y + before_y + after_z + before_z
                speed[x] = total * (1.0 / 7.0)
            return carry

        lax.fori_loop(0, rows_x // step, body, 0)

    blocks_x, blocks_y, blocks_z = band.shape
    wide_x, wide_y, wide_z = rows_x // blocks_x, rows_y // blocks_y, depth // blocks_z
    lane_row = lax.broadcasted_iota(jnp.int32, (wide_y, depth), 1)

    def advance(f, store):
        for p in range(blocks_x):
            strips = []
            for q in range(blocks_y):
                strip = jnp.zeros((wide_y, depth), F32)
                for r in range(blocks_z):
                    entry = band[p, q, r].astype(F32) * time_step[0]
                    strip = jnp.where((lane_row >= r * wide_z) & (lane_row < (r + 1) * wide_z), entry, strip)
                strips.append(strip)
            step_size = jnp.concatenate(strips, axis=0)

            step = divisor(wide_x, 4)

            def body(i, carry):
                for u in range(step):
                    x = p * wide_x + i * step + u
                    after_y, before_y = around_y(grad[1, x + 1])
                    after_z, before_z = around_z(grad[2, x + 1, :rows_y])
                    curvature = 0.5 * (
                        (grad[0, x + 2, :rows_y] - grad[0, x, :rows_y])
                        + (after_y - before_y) + (after_z - before_z)
                    )
                    phi = field[f, HALO + x, own_y]
                    store(x, phi - step_size * mag[x + 1, :rows_y] * (speed[x] - 0.5 * curvature))
                return carry

            lax.fori_loop(0, wide_x // step, body, 0)

    def store_next(x, value):
        field[2, HALO + x, own_y] = value

    def store_out(x, value):
        out[x] = value

    local[0].wait()
    arrived(0, mains)
    own_planes(0)
    local[1].wait()
    arrived(0, edges[0])
    start(0, corners[0])
    own_gradients()
    arrived(0, edges[1])
    start(0, corners[1])
    arrived(1, mains)
    own_planes(1)
    own_velocity()
    arrived(0, corners[0])
    halo_planes(0, 0)
    arrived(0, corners[1])
    halo_planes(0, 1)
    normals()
    for n in range(2):
        arrived(1, edges[n])
        start(1, corners[n])
    for n in range(2):
        arrived(1, corners[n])
        halo_planes(1, n)
    velocity()
    speeds()
    advance(0, store_next)
    start(2, edges[0] + mains + edges[1])
    arrived(2, mains)
    own_planes(2)
    own_gradients()
    for n in range(2):
        arrived(2, edges[n])
        start(2, corners[n])
    for n in range(2):
        arrived(2, corners[n])
        halo_planes(2, n)
    normals()
    advance(2, store_out)
    for f in range(3):
        sent(f, mains + edges[0] + edges[1] + corners[0] + corners[1])


def per_device(nx, ny, level_set, sensitivity, smooth_taps, slope_taps, band, time_step):
    rows_x, rows_y, depth = level_set.shape
    ext_x = rows_x + 2 * HALO
    ext_y = rows_y + 2 * SIDE
    out_y = rows_y + 8
    smem = pl.BlockSpec(memory_space=pltpu.SMEM)
    hbm = pl.BlockSpec(memory_space=pl.ANY)
    return pl.pallas_call(
        functools.partial(kernel, nx, ny),
        out_shape=jax.ShapeDtypeStruct(level_set.shape, F32),
        in_specs=[smem, smem, smem, smem, hbm, hbm],
        out_specs=pl.BlockSpec(memory_space=pltpu.VMEM),
        scratch_shapes=[
            pltpu.VMEM((3, ext_x, ext_y, depth), F32),
            pltpu.VMEM((4, ext_x, out_y, depth), F32),
            pltpu.VMEM((3, rows_x + 2, out_y, depth), F32),
            pltpu.VMEM((rows_x + 2, out_y, depth), F32),
            pltpu.VMEM((rows_x + 2, out_y, depth), F32),
            pltpu.VMEM((rows_x, rows_y, depth), F32),
            pltpu.VMEM((3 * depth, 2 * depth), BF16),
            pltpu.VMEM((2 * out_y, 3 * ext_y), BF16),
            pltpu.SemaphoreType.DMA((3, 14)),
            pltpu.SemaphoreType.DMA((3, 14)),
            pltpu.SemaphoreType.DMA((2,)),
        ],
        compiler_params=pltpu.CompilerParams(
            collective_id=0, has_side_effects=True,
        ),
        name="level_set_updates",
    )(smooth_taps, slope_taps, band, time_step, level_set, sensitivity)


def solution(mesh):
    return jax.shard_map(
        functools.partial(per_device, mesh.shape["gx"], mesh.shape["gy"]),
        mesh=mesh,
        in_specs=(P("gx", "gy", None), P("gx", "gy", None), P(), P(), P("gx", "gy", None), P()),
        out_specs=P("gx", "gy", None),
        check_vma=False,
    )
```

```python
import functools

import jax
import jax.numpy as jnp
from jax import lax
from jax.experimental import pallas as pl
from jax.experimental.pallas import tpu as pltpu
from jax.sharding import PartitionSpec as P

UPDATES = 2
TAPS = 25
REACH = TAPS // 2
HALO = REACH + 1
SIDE = 16
F32 = jnp.float32
BF16 = jnp.bfloat16
MESH = pl.DeviceIdType.MESH


def split(value):
    high = value.astype(BF16)
    low = (value - high.astype(F32)).astype(BF16)
    return high, low


def toeplitz(offset, keep, taps):
    out = jnp.zeros(offset.shape, F32)
    for k in range(TAPS):
        out = jnp.where(offset == k, taps[k], out)
    if keep is not None:
        out = jnp.where(keep, out, 0.0)
    return out


def divisor(count, limit):
    return max(d for d in range(1, limit + 1) if count % d == 0)


def kernel(
    nx, ny,
    smooth, slope, band, time_step, phi_hbm, sens_hbm,
    out,
    field, part, grad, mag, vel, speed, zmat, ymat,
    send_sem, recv_sem, local_sem,
):
    rows_x, rows_y, depth = out.shape
    ext_x = rows_x + 2 * HALO
    ext_y = rows_y + 2 * SIDE
    out_y = rows_y + 8
    px = lax.axis_index("gx")
    py = lax.axis_index("gy")
    has = {
        "x-": px > 0, "x+": px < nx - 1, "y-": py > 0, "y+": py < ny - 1,
    }
    peer = {
        "x-": (px - 1, py), "x+": (px + 1, py), "y-": (px, py - 1), "y+": (px, py + 1),
    }
    opposite = {"x-": "x+", "x+": "x-", "y-": "y+", "y+": "y-"}
    own_x = pl.ds(HALO, rows_x)
    own_y = pl.ds(SIDE, rows_y)
    low_x, high_x = pl.ds(0, HALO), pl.ds(HALO + rows_x, HALO)
    low_y, high_y = pl.ds(0, SIDE), pl.ds(SIDE + rows_y, SIDE)

    barrier = pltpu.get_barrier_semaphore()
    for side in has:
        @pl.when(has[side])
        def _(side=side):
            pl.semaphore_signal(barrier, inc=1, device_id=peer[side], device_id_type=MESH)

    local = [
        pltpu.make_async_copy(source, field.at[f, own_x, own_y], local_sem.at[f])
        for f, source in enumerate((phi_hbm, sens_hbm))
    ]
    for copy in local:
        copy.start()

    def source_of(f, xs, ys):
        if f == 2:
            return field.at[f, pl.ds(HALO + xs[0], xs[1]), pl.ds(SIDE + ys[0], ys[1])]
        return (phi_hbm, sens_hbm)[f].at[pl.ds(xs[0], xs[1]), pl.ds(ys[0], ys[1])]

    cut = HALO - HALO // 2
    pieces = ((0, cut), (cut, HALO - cut))
    first_x = {"x-": 0, "x+": HALO + rows_x}
    mains = (0, 1)
    edges = tuple((2 + 6 * n, 3 + 6 * n) for n in range(2))
    corners = tuple(tuple(range(4 + 6 * n, 8 + 6 * n)) for n in range(2))

    def remote(f, kind):
        there = None
        if kind in mains:
            side = ("y+", "y-")[kind]
            ys = (rows_y - SIDE, SIDE) if side == "y+" else (0, SIDE)
            src = source_of(f, (0, rows_x), ys)
            dst = field.at[f, own_x, low_y if side == "y+" else high_y]
        else:
            at, size = pieces[(kind - 2) // 6]
            which = (kind - 2) % 6
            if which < 2:
                side = ("x+", "x-")[which]
                begin = rows_x - HALO + at if side == "x+" else at
                src = source_of(f, (begin, size), (0, rows_y))
                dst = field.at[f, pl.ds(first_x[opposite[side]] + at, size), own_y]
            else:
                side = ("y+", "y-")[(which - 2) // 2]
                there = ("x-", "x+")[(which - 2) % 2]
                xs = pl.ds(first_x[there] + at, size)
                src = field.at[f, xs, pl.ds(rows_y if side == "y+" else SIDE, SIDE)]
                dst = field.at[f, xs, low_y if side == "y+" else high_y]
        copy = pltpu.make_async_remote_copy(
            src_ref=src, dst_ref=dst,
            send_sem=send_sem.at[f, kind], recv_sem=recv_sem.at[f, kind],
            device_id=peer[side], device_id_type=MESH,
        )
        sends, receives = has[side], has[opposite[side]]
        if there is not None:
            sends, receives = sends & has[there], receives & has[there]
        return copy, sends, receives

    def start(f, kinds):
        for kind in kinds:
            copy, sends, _ = remote(f, kind)
            pl.when(sends)(copy.start)

    def arrived(f, kinds):
        for kind in kinds:
            copy, _, receives = remote(f, kind)
            pl.when(receives)(copy.wait_recv)

    def sent(f, kinds):
        for kind in kinds:
            copy, sends, _ = remote(f, kind)
            pl.when(sends)(copy.wait_send)

    neighbours = sum(has[side].astype(jnp.int32) for side in has)
    pl.semaphore_wait(barrier, neighbours)
    for f in range(2):
        start(f, edges[0] + mains + edges[1])

    for f in range(3):
        @pl.when(px == 0)
        def _(f=f):
            field[f, low_x] = jnp.zeros((HALO, ext_y, depth), F32)

        @pl.when(px == nx - 1)
        def _(f=f):
            field[f, high_x] = jnp.zeros((HALO, ext_y, depth), F32)

        @pl.when(py == 0)
        def _(f=f):
            field[f, :, low_y] = jnp.zeros((ext_x, SIDE, depth), F32)

        @pl.when(py == ny - 1)
        def _(f=f):
            field[f, :, high_y] = jnp.zeros((ext_x, SIDE, depth), F32)

    offset = (
        lax.broadcasted_iota(jnp.int32, (depth, depth), 0)
        - lax.broadcasted_iota(jnp.int32, (depth, depth), 1) + REACH
    )
    for n, taps in enumerate((smooth, slope)):
        high, low = split(toeplitz(offset, None, taps))
        cols = pl.ds(n * depth, depth)
        zmat[pl.ds(0, depth), cols] = high
        zmat[pl.ds(depth, depth), cols] = high
        zmat[pl.ds(2 * depth, depth), cols] = low
    row = lax.broadcasted_iota(jnp.int32, (out_y, ext_y), 0)
    cell = jnp.where(row == out_y - 1, -1, row)
    keep = (cell <= rows_y) & ((cell >= 0) | (py > 0)) & ((cell < rows_y) | (py < ny - 1))
    offset = lax.broadcasted_iota(jnp.int32, (out_y, ext_y), 1) - cell - (SIDE - REACH)
    strips = []
    for taps in (smooth, slope):
        high, low = split(toeplitz(offset, keep, taps))
        strips.append(jnp.concatenate([high.astype(F32), high.astype(F32), low.astype(F32)], axis=1))
    ymat[...] = jnp.concatenate(strips, axis=0).astype(BF16)

    def planes(f, first, count):
        high, low = split(field[f, pl.ds(first, count)].reshape(count * ext_y, depth))
        lhs = jnp.concatenate([high, low, high], axis=1)
        width = depth if f == 1 else 2 * depth
        high, low = split(jnp.dot(lhs, zmat[:, :width], preferred_element_type=F32))

        def stack(r):
            rows = slice(r * ext_y, (r + 1) * ext_y)
            return jnp.concatenate([high[rows], low[rows], high[rows]], axis=0)

        if f == 1:
            for r in range(0, count, 2):
                both = [stack(q) for q in range(r, min(r + 2, count))]
                y_out = jnp.dot(ymat[:out_y], jnp.concatenate(both, axis=1), preferred_element_type=F32)
                for q in range(len(both)):
                    part[3, first + r + q] = y_out[:, q * depth:(q + 1) * depth]
        else:
            for r in range(count):
                y_out = jnp.dot(ymat[...], stack(r), preferred_element_type=F32)
                part[0, first + r] = y_out[:out_y, :depth]
                part[1, first + r] = y_out[out_y:, :depth]
                part[2, first + r] = y_out[:out_y, depth:]

    def own_planes(f):
        step = divisor(rows_x, 16)

        def body(i, carry):
            planes(f, HALO + i * step, step)
            return carry

        lax.fori_loop(0, rows_x // step, body, 0)

    def halo_planes(f, n):
        at, size = pieces[n]

        def body(i, carry):
            planes(f, i * (HALO + rows_x) + at, size)
            return carry

        lax.fori_loop(0, 2, body, 0)

    group = divisor(rows_x + 2, 17)
    tiles = out_y // 8

    def is_own(row):
        return HALO <= row < HALO + rows_x

    def smooth_x(n, first, rows, own, target):
        acc = [None] * group
        for j in range(group + TAPS - 1):
            if is_own(first + j) != own:
                continue
            value = part[n, first + j, rows]
            for g in range(max(0, j - TAPS + 1), min(group, j + 1)):
                term = smooth[j - g] * value
                acc[g] = term if acc[g] is None else acc[g] + term
        return finish(acc, first, rows, own, target)

    def finish(acc, first, rows, own, target):
        if own:
            for g in range(group):
                target(first + g, rows, acc[g])
            return None
        return acc

    def slope_x(n, first, rows, own, target):
        values = {
            j: part[n, first + j, rows]
            for j in range(group + TAPS - 1) if is_own(first + j) == own
        }
        acc = []
        for g in range(group):
            total = None
            for k in range(REACH + 1, TAPS):
                after, before = values.get(g + k), values.get(g + TAPS - 1 - k)
                if after is None and before is None:
                    continue
                if before is None:
                    pair = after
                elif after is None:
                    pair = -before
                else:
                    pair = after - before
                term = slope[k] * pair
                total = term if total is None else total + term
            acc.append(total)
        return finish(acc, first, rows, own, target)

    def each_tile(work):
        for first in range(0, rows_x + 2, group):
            def body(i, carry, first=first):
                work(first, pl.ds(pl.multiple_of(i * 8, 8), 8))
                return carry

            lax.fori_loop(0, tiles, body, 0)

    def plus(ref_value, extra):
        return ref_value if extra is None else ref_value + extra

    def put_grad(n):
        def target(x, rows, value):
            grad[n, x, rows] = jnp.zeros((8, depth), F32) if value is None else value
        return target

    def put_vel(x, rows, value):
        vel[x, rows] = jnp.zeros((8, depth), F32) if value is None else value

    def own_gradients():
        def work(first, rows):
            slope_x(0, first, rows, True, put_grad(0))
            smooth_x(1, first, rows, True, put_grad(1))
            smooth_x(2, first, rows, True, put_grad(2))

        each_tile(work)

    def normals():
        def work(first, rows):
            more_x = slope_x(0, first, rows, False, None)
            more_y = smooth_x(1, first, rows, False, None)
            more_z = smooth_x(2, first, rows, False, None)
            for g in range(group):
                gx = plus(grad[0, first + g, rows], more_x[g])
                gy = plus(grad[1, first + g, rows], more_y[g])
                gz = plus(grad[2, first + g, rows], more_z[g])
                square = gx * gx + gy * gy + gz * gz + 1.0
                inverse = lax.rsqrt(square)
                grad[0, first + g, rows] = gx * inverse
                grad[1, first + g, rows] = gy * inverse
                grad[2, first + g, rows] = gz * inverse
                mag[first + g, rows] = square * inverse

        each_tile(work)
        for edge, at in ((px == 0, 0), (px == nx - 1, rows_x + 1)):
            @pl.when(edge)
            def _(at=at):
                grad[0, at] = jnp.zeros((out_y, depth), F32)

    def own_velocity():
        each_tile(lambda first, rows: smooth_x(3, first, rows, True, put_vel))

    def velocity():
        def work(first, rows):
            for g, extra in enumerate(smooth_x(3, first, rows, False, None)):
                if extra is not None:
                    vel[first + g, rows] = vel[first + g, rows] + extra

        each_tile(work)
        for edge, at in ((px == 0, 0), (px == nx - 1, rows_x + 1)):
            @pl.when(edge)
            def _(at=at):
                vel[at] = jnp.zeros((out_y, depth), F32)

    lane = lax.broadcasted_iota(jnp.int32, (rows_y, depth), 1)

    def around_y(value):
        after = pltpu.roll(value, out_y - 1, 0)[:rows_y]
        before = pltpu.roll(value, 1, 0)[:rows_y]
        return after, before

    def around_z(value):
        after = jnp.where(lane == depth - 1, 0.0, pltpu.roll(value, depth - 1, 1))
        before = jnp.where(lane == 0, 0.0, pltpu.roll(value, 1, 1))
        return after, before

    def speed_at(x):
        value = vel[x + 1]
        after_y, before_y = around_y(value)
        inner = value[:rows_y]
        after_z, before_z = around_z(inner)
        total = inner + vel[x + 2, :rows_y] + vel[x, :rows_y]
        total = total + after_y + before_y + after_z + before_z
        total = total * (1.0 / 7.0)
        speed[x] = total
        return total

    blocks_x, blocks_y, blocks_z = band.shape
    wide_x, wide_y, wide_z = rows_x // blocks_x, rows_y // blocks_y, depth // blocks_z
    lane_row = lax.broadcasted_iota(jnp.int32, (wide_y, depth), 1)

    def advance(f, speed_of, store, after):
        for p in range(blocks_x):
            strips = []
            for q in range(blocks_y):
                strip = jnp.zeros((wide_y, depth), F32)
                for r in range(blocks_z):
                    entry = band[p, q, r].astype(F32) * time_step[0]
                    strip = jnp.where((lane_row >= r * wide_z) & (lane_row < (r + 1) * wide_z), entry, strip)
                strips.append(strip)
            step_size = jnp.concatenate(strips, axis=0)

            step = divisor(wide_x, 4)

            def body(i, carry):
                for u in range(step):
                    x = p * wide_x + i * step + u
                    after_y, before_y = around_y(grad[1, x + 1])
                    after_z, before_z = around_z(grad[2, x + 1, :rows_y])
                    curvature = 0.5 * (
                        (grad[0, x + 2, :rows_y] - grad[0, x, :rows_y])
                        + (after_y - before_y) + (after_z - before_z)
                    )
                    phi = field[f, HALO + x, own_y]
                    store(x, phi - step_size * mag[x + 1, :rows_y] * (speed_of(x) - 0.5 * curvature))
                return carry

            lax.fori_loop(0, wide_x // step, body, 0)
            after(p)

    def store_next(x, value):
        field[2, HALO + x, own_y] = value

    def store_out(x, value):
        out[x] = value

    local[0].wait()
    arrived(0, mains)
    own_planes(0)
    local[1].wait()
    arrived(0, edges[0])
    start(0, corners[0])
    own_gradients()
    arrived(0, edges[1])
    start(0, corners[1])
    arrived(1, mains)
    own_planes(1)
    own_velocity()
    arrived(0, corners[0])
    halo_planes(0, 0)
    arrived(0, corners[1])
    halo_planes(0, 1)
    normals()
    for n in range(2):
        arrived(1, edges[n])
        start(1, corners[n])
    for n in range(2):
        arrived(1, corners[n])
        halo_planes(1, n)
    velocity()

    low_done = -(-HALO // wide_x) - 1

    def send_next(p):
        if p == low_done:
            start(2, (edges[0][1], edges[1][1]))
        if p == blocks_x - 1:
            start(2, (edges[0][0],) + mains + (edges[1][0],))

    advance(0, speed_at, store_next, send_next)
    arrived(2, mains)
    own_planes(2)
    own_gradients()
    for n in range(2):
        arrived(2, edges[n])
        start(2, corners[n])
    for n in range(2):
        arrived(2, corners[n])
        halo_planes(2, n)
    normals()
    advance(2, lambda x: speed[x], store_out, lambda p: None)
    for f in range(3):
        sent(f, mains + edges[0] + edges[1] + corners[0] + corners[1])


def per_device(nx, ny, level_set, sensitivity, smooth_taps, slope_taps, band, time_step):
    rows_x, rows_y, depth = level_set.shape
    ext_x = rows_x + 2 * HALO
    ext_y = rows_y + 2 * SIDE
    out_y = rows_y + 8
    smem = pl.BlockSpec(memory_space=pltpu.SMEM)
    hbm = pl.BlockSpec(memory_space=pl.ANY)
    return pl.pallas_call(
        functools.partial(kernel, nx, ny),
        out_shape=jax.ShapeDtypeStruct(level_set.shape, F32),
        in_specs=[smem, smem, smem, smem, hbm, hbm],
        out_specs=pl.BlockSpec(memory_space=pltpu.VMEM),
        scratch_shapes=[
            pltpu.VMEM((3, ext_x, ext_y, depth), F32),
            pltpu.VMEM((4, ext_x, out_y, depth), F32),
            pltpu.VMEM((3, rows_x + 2, out_y, depth), F32),
            pltpu.VMEM((rows_x + 2, out_y, depth), F32),
            pltpu.VMEM((rows_x + 2, out_y, depth), F32),
            pltpu.VMEM((rows_x, rows_y, depth), F32),
            pltpu.VMEM((3 * depth, 2 * depth), BF16),
            pltpu.VMEM((2 * out_y, 3 * ext_y), BF16),
            pltpu.SemaphoreType.DMA((3, 14)),
            pltpu.SemaphoreType.DMA((3, 14)),
            pltpu.SemaphoreType.DMA((2,)),
        ],
        compiler_params=pltpu.CompilerParams(
            collective_id=0, has_side_effects=True,
        ),
        name="level_set_updates",
    )(smooth_taps, slope_taps, band, time_step, level_set, sensitivity)


def solution(mesh):
    return jax.shard_map(
        functools.partial(per_device, mesh.shape["gx"], mesh.shape["gy"]),
        mesh=mesh,
        in_specs=(P("gx", "gy", None), P("gx", "gy", None), P(), P(), P("gx", "gy", None), P()),
        out_specs=P("gx", "gy", None),
        check_vma=False,
    )
```
